32 devices in a mesh: half: 2 (over y), row: 4 (over z), col: 4 (over x, core).
Axes of the slice: x: 2, y: 2, z: 4, core: 2. Of those that a mesh axis runs over, the one named last changes fastest.
Arguments:
- front_init: float32 [10240, 10240], P(('half', 'row'), 'col'), may hold values from -2 to 8, as said below
- child_update: float32 [2, 8192, 8192], P('half', 'row', 'col'), may hold values from -2 to 8, as said below
- child_map: int32 [2, 8192], replicated, may hold values from 0 to 10239, as said below
Outputs:
- factor_front: float32 [10240, 10240], P(('half', 'row'), 'col')
The draws below stay inside these ranges and needn't reach their ends.
Inputs may be any that keep to these rules, and one draw needn't show every extreme that they name: `child_map`: each child's entries are distinct. Each aligned block of 128 child indices maps onto one whole block of 128 front indices; write b(j) for the front block of child block j. For every r and q below 4, exactly 4 child blocks j with j % 4 == r have b(j) % 4 == q, and these share one value of b(j) % 8. Symmetric in natural order, and front_init minus the identity is positive semidefinite. `child_update`: each child's matrix is symmetric positive semidefinite.
All inputs are finite; a program needn't handle non-finite values.
Results may differ from the reference program's by a relative error of at most 0.0001.
Values sent between devices are 32-bit elements; how exact they have to be, the bound alone decides.
A program may use at most 256 MiB of HBM per device.

```python
import jax
import jax.numpy as jnp
from jax import lax

F = 10240
UC = 8192
BLOCK_EDGE = 128
PANELS = 2
DEVICE_GRID = 4
HALVES = 2
ROW_GROUPS = 8
GROUP_ROWS = 10
FRONT_COLUMNS = 20
CRB = 16
CB = 64
CAP = 4
PANEL = 256


def rough_matrix(key, rows, cols):
    return jnp.clip(jax.random.normal(key, (rows, cols), jnp.float32), -5.0, 5.0)


def gram_matrix(key, order, rank_width):
    subkeys = jax.random.split(key, 1)
    factor_rows = rough_matrix(subkeys[0], order, rank_width)
    product = jnp.dot(factor_rows, factor_rows.T, precision=lax.Precision.HIGHEST) / rank_width
    return (product + product.T) * 0.5


def draw_front_init(key, part):
    gram = gram_matrix(jax.random.fold_in(key, 301), F, F // 10)
    natural_order = gram + jnp.eye(F, dtype=jnp.float32)
    reshaped_front = natural_order.reshape(GROUP_ROWS, ROW_GROUPS, BLOCK_EDGE, FRONT_COLUMNS, DEVICE_GRID, BLOCK_EDGE)
    return reshaped_front.transpose(1, 0, 2, 4, 3, 5).reshape(F, F)


def draw_child_update(key, part):
    results = []
    for which_child in range(2):
        results.append(gram_matrix(jax.random.fold_in(key, 401 + which_child), UC, UC // 8))
    return jnp.stack(results)


def one_child_map(key):
    subkeys = jax.random.split(key, 4)
    per_half = GROUP_ROWS // CAP
    slot_total = HALVES * per_half
    chosen = jax.vmap(lambda subkey: jax.random.permutation(subkey, slot_total)[:DEVICE_GRID])(jax.random.split(subkeys[0], DEVICE_GRID))
    within = jax.vmap(lambda subkey: jax.random.permutation(subkey, GROUP_ROWS))(jax.random.split(subkeys[1], DEVICE_GRID * HALVES))
    within = within.reshape(DEVICE_GRID, HALVES, GROUP_ROWS)
    half_pick = chosen // per_half
    offset = chosen % per_half
    picked_rows = within[jnp.arange(DEVICE_GRID)[:, None], half_pick]
    positions = offset[:, :, None] * CAP + jnp.arange(CAP)[None, None, :]
    block_rows = jnp.take_along_axis(picked_rows, positions, axis=2)
    front_block = (half_pick * DEVICE_GRID + jnp.arange(DEVICE_GRID)[:, None])[:, :, None] + ROW_GROUPS * block_rows
    by_row = front_block.transpose(1, 0, 2).reshape(DEVICE_GRID, DEVICE_GRID * CAP)
    local_order = jax.vmap(lambda subkey: jax.random.permutation(subkey, DEVICE_GRID * CAP))(jax.random.split(subkeys[2], DEVICE_GRID))
    placed = jnp.zeros((DEVICE_GRID, DEVICE_GRID * CAP), jnp.int32).at[jnp.arange(DEVICE_GRID)[:, None], local_order].set(by_row.astype(jnp.int32))
    block_map = placed.T.reshape(CB)
    inner_perm = jax.vmap(lambda subkey: jax.random.permutation(subkey, BLOCK_EDGE))(jax.random.split(subkeys[3], CB))
    return (block_map[:, None] * BLOCK_EDGE + inner_perm).reshape(UC).astype(jnp.int32)


def draw_child_map(key, part):
    return jnp.stack([one_child_map(jax.random.fold_in(key, 501 + which_child)) for which_child in range(2)])


def setup_inputs(seed: int = 0) -> dict:
    keys = jax.random.split(jax.random.key(seed), 4)
    return {
        "front_init": draw_front_init(jax.random.fold_in(keys[3], 71), 0),
        "child_update": draw_child_update(jax.random.fold_in(keys[3], 71), 0),
        "child_map": draw_child_map(jax.random.fold_in(keys[3], 71), 0),
    }


def front_natural(stored_layout):
    reshaped_front = stored_layout.reshape(ROW_GROUPS, GROUP_ROWS, BLOCK_EDGE, DEVICE_GRID, FRONT_COLUMNS, BLOCK_EDGE)
    return reshaped_front.transpose(1, 0, 2, 4, 3, 5).reshape(F, F)

def front_stored(natural_order):
    reshaped_front = natural_order.reshape(GROUP_ROWS, ROW_GROUPS, BLOCK_EDGE, FRONT_COLUMNS, DEVICE_GRID, BLOCK_EDGE)
    return reshaped_front.transpose(1, 0, 2, 4, 3, 5).reshape(F, F)

def child_natural(stored_layout):
    reshaped_front = stored_layout.reshape(DEVICE_GRID, CRB, BLOCK_EDGE, DEVICE_GRID, CRB, BLOCK_EDGE)
    return reshaped_front.transpose(1, 0, 2, 4, 3, 5).reshape(UC, UC)

def reference(front_init, child_update, child_map):
    front_local = front_natural(front_init)
    for which_child in range(2):
        update = child_natural(child_update[which_child])
        targets = child_map[which_child]
        spread = jnp.zeros((UC, F), jnp.float32).at[:, targets].set(update)
        front_local = front_local.at[targets].add(spread)
    identity = jnp.eye(PANEL, dtype=jnp.float32)
    row_ids = jnp.arange(F)
    for panel_index in range(PANELS):
        panel_start = panel_index * PANEL
        panel_end = panel_start + PANEL
        factor = jnp.linalg.cholesky(front_local[panel_start:panel_end, panel_start:panel_end])
        inverse = lax.linalg.triangular_solve(factor, identity, left_side=True, lower=True)
        lower_rows = jnp.dot(front_local[:, panel_start:panel_end], inverse.T, precision=lax.Precision.HIGHEST)
        lower_rows = jnp.where((row_ids >= panel_start)[:, None], lower_rows, 0.0)
        tail_rows = lower_rows[panel_end:]
        update = jnp.dot(tail_rows, tail_rows.T, precision=lax.Precision.HIGHEST)
        front_local = front_local.at[panel_end:, panel_end:].set(front_local[panel_end:, panel_end:] - update)
        front_local = front_local.at[:, panel_start:panel_end].set(lower_rows)
        front_local = front_local.at[panel_start:panel_end, panel_end:].set(0.0)
    return front_stored(front_local)
```

```python
import functools

import jax
import jax.numpy as jnp
from jax import lax
from jax.experimental import pallas as pl
from jax.experimental.pallas import tpu as pltpu
from jax.sharding import PartitionSpec as P

BE = 128
PANEL = 256
WIDE = 512
HIGHEST = lax.Precision.HIGHEST
F32 = jnp.float32
BF16 = jnp.bfloat16


def absdiff(a, b):
    return jnp.maximum(a - b, b - a)


def use_direct(a, b, x, y):
    direct = 2 * absdiff(a, x) + absdiff(b // 2, y // 2)
    swapped = 2 * absdiff(b, x) + absdiff(a // 2, y // 2)
    return direct <= swapped


def pack_kernel(grid_size, slots, row_order, col_order, src, dst):
    for y in range(grid_size):
        for k in range(slots):
            at = pl.multiple_of(col_order[y * slots + k] * BE, BE)
            dst[0, y, :, k * BE : (k + 1) * BE] = src[:, pl.ds(at, BE)]


def pack(child, row_order, col_order, grid_size, slots):
    rows, cols = child.shape
    side = slots * BE
    return pl.pallas_call(
        functools.partial(pack_kernel, grid_size, slots),
        grid_spec=pltpu.PrefetchScalarGridSpec(
            num_scalar_prefetch=2,
            grid=(grid_size * slots,),
            in_specs=[pl.BlockSpec((BE, cols), lambda n, ro, co: (ro[n], 0))],
            out_specs=pl.BlockSpec(
                (1, grid_size, BE, side), lambda n, ro, co: (n // slots, 0, n % slots, 0)
            ),
        ),
        out_shape=jax.ShapeDtypeStruct((grid_size, grid_size, side, side), F32),
    )(row_order, col_order, child)


def exchange_kernel(grid_size, src, dst, send_direct, send_swap, recv, local):
    r = lax.axis_index("row")
    s = lax.axis_index("col")
    half = lax.axis_index("half")
    g = grid_size

    def peer(k):
        return (r + k // g) % g, (s + k % g) % g

    barrier = pltpu.get_barrier_semaphore()

    def greet(k, carry):
        x, y = peer(k)
        pl.semaphore_signal(
            barrier, inc=1, device_id=(half, x, y), device_id_type=pl.DeviceIdType.MESH
        )
        return carry

    lax.fori_loop(1, g * g, greet, 0)
    pl.semaphore_wait(barrier, g * g - 1)

    own = pltpu.make_async_copy(src.at[r, s], dst.at[r, s], local.at[0])
    own_swap = pltpu.make_async_copy(src.at[s, r], dst.at[s, r], local.at[1])
    own.start()

    @pl.when(r != s)
    def _():
        own_swap.start()

    def direct_copy(k, x, y):
        return pltpu.make_async_remote_copy(
            src_ref=src.at[x, y],
            dst_ref=dst.at[r, s],
            send_sem=send_direct.at[k],
            recv_sem=recv.at[r * g + s],
            device_id=(half, x, y),
            device_id_type=pl.DeviceIdType.MESH,
        )

    def swap_copy(k, x, y):
        return pltpu.make_async_remote_copy(
            src_ref=src.at[y, x],
            dst_ref=dst.at[s, r],
            send_sem=send_swap.at[k],
            recv_sem=recv.at[s * g + r],
            device_id=(half, x, y),
            device_id_type=pl.DeviceIdType.MESH,
        )

    def send(k, carry):
        x, y = peer(k)

        @pl.when(use_direct(r, s, x, y))
        def _():
            direct_copy(k, x, y).start()

        @pl.when(jnp.logical_not(use_direct(s, r, x, y)))
        def _():
            swap_copy(k, x, y).start()

        return carry

    lax.fori_loop(1, g * g, send, 0)

    def sent(k, carry):
        x, y = peer(k)

        @pl.when(use_direct(r, s, x, y))
        def _():
            direct_copy(k, x, y).wait_send()

        @pl.when(jnp.logical_not(use_direct(s, r, x, y)))
        def _():
            swap_copy(k, x, y).wait_send()

        return carry

    lax.fori_loop(1, g * g, sent, 0)

    def arrived(k, carry):
        a = k // g
        b = k % g
        mine = jnp.logical_or(
            jnp.logical_and(a == r, b == s), jnp.logical_and(a == s, b == r)
        )

        @pl.when(jnp.logical_not(mine))
        def _():
            pltpu.make_async_remote_copy(
                src_ref=src.at[a, b],
                dst_ref=dst.at[a, b],
                send_sem=send_direct.at[0],
                recv_sem=recv.at[k],
                device_id=(half, (r + 1) % g, s),
                device_id_type=pl.DeviceIdType.MESH,
            ).wait_recv()

        return carry

    lax.fori_loop(0, g * g, arrived, 0)
    own.wait()

    @pl.when(r != s)
    def _():
        own_swap.wait()


def exchange(packed, grid_size):
    n = grid_size * grid_size
    return pl.pallas_call(
        functools.partial(exchange_kernel, grid_size),
        out_shape=jax.ShapeDtypeStruct(packed.shape, F32),
        in_specs=[pl.BlockSpec(memory_space=pl.ANY)],
        out_specs=pl.BlockSpec(memory_space=pl.ANY),
        scratch_shapes=[
            pltpu.SemaphoreType.DMA((n,)),
            pltpu.SemaphoreType.DMA((n,)),
            pltpu.SemaphoreType.DMA((n,)),
            pltpu.SemaphoreType.DMA((2,)),
        ],
        compiler_params=pltpu.CompilerParams(collective_id=0, has_side_effects=True),
    )(packed)


def place_kernel(
    grid_size, slots, steps, chunk_at, t_at, u_at, swapped, valid,
    front, chunk, row_perm, col_perm, out, acc, work, mid, sem,
):
    n = pl.program_id(0)
    a = n // grid_size
    s = n % grid_size

    @pl.when(n == 0)
    def _():
        load = pltpu.make_async_copy(front, acc, sem)
        load.start()
        load.wait()

    @pl.when(valid[a] == 1)
    def _():
        @pl.when(swapped[n] == 1)
        def _():
            work[...] = chunk[0].T

        @pl.when(swapped[n] == 0)
        def _():
            work[...] = chunk[0]

        for i in range(slots):
            t = pl.multiple_of(t_at[a * slots + i] * BE, BE)
            part = work[i * BE : (i + 1) * BE, :]
            high = part.astype(BF16)
            low = (part - high.astype(F32)).astype(BF16)
            perm = row_perm[0, i]
            mid[0] = jnp.dot(perm, high, preferred_element_type=F32).astype(BF16)
            mid[1] = jnp.dot(perm, low, preferred_element_type=F32).astype(BF16)
            for k in range(slots):
                u = pl.multiple_of(u_at[s * slots + k] * BE, BE)
                lanes = slice(k * BE, (k + 1) * BE)
                both = jnp.concatenate([mid[0, :, lanes], mid[1, :, lanes]], axis=1)
                perm2 = jnp.concatenate([col_perm[0, k], col_perm[0, k]], axis=0)
                acc[pl.ds(t, BE), pl.ds(u, BE)] += jnp.dot(
                    both, perm2, preferred_element_type=F32
                )

    @pl.when(n == steps - 1)
    def _():
        store = pltpu.make_async_copy(acc, out, sem)
        store.start()
        store.wait()


def place(front, chunks, chunk_at, t_at, u_at, swapped, valid, row_perm, col_perm, grid_size):
    slots = row_perm.shape[1]
    steps = row_perm.shape[0] * grid_size
    side = slots * BE
    return pl.pallas_call(
        functools.partial(place_kernel, grid_size, slots, steps),
        grid_spec=pltpu.PrefetchScalarGridSpec(
            num_scalar_prefetch=5,
            grid=(steps,),
            in_specs=[
                pl.BlockSpec(memory_space=pl.ANY),
                pl.BlockSpec((1, side, side), lambda n, ca, *_: (ca[n], 0, 0)),
                pl.BlockSpec((1, slots, BE, BE), lambda n, *_: (n // grid_size, 0, 0, 0)),
                pl.BlockSpec((1, slots, BE, BE), lambda n, *_: (n % grid_size, 0, 0, 0)),
            ],
            out_specs=pl.BlockSpec(memory_space=pl.ANY),
            scratch_shapes=[
                pltpu.VMEM(front.shape, F32),
                pltpu.VMEM((side, side), F32),
                pltpu.VMEM((2, BE, side), BF16),
                pltpu.SemaphoreType.DMA,
            ],
        ),
        out_shape=jax.ShapeDtypeStruct(front.shape, F32),
        compiler_params=pltpu.CompilerParams(vmem_limit_bytes=40 * 1024 * 1024),
        cost_estimate=pl.CostEstimate(
            flops=4_000_000_000, bytes_accessed=36_000_000, transcendentals=0
        ),
    )(chunk_at, t_at, u_at, swapped, valid, front, chunks, row_perm, col_perm)


def update_kernel(place_of, front, lrow, lcol, out, col_high, col_low):
    t = pl.program_id(0)
    dims = (((1,), (1,)), ((), ()))

    @pl.when(t == 0)
    def _():
        whole = lcol[...]
        high = whole.astype(BF16)
        col_high[...] = high
        col_low[...] = (whole - high.astype(F32)).astype(BF16)

    rows = lrow[...]
    high = rows.astype(BF16)
    low = (rows - high.astype(F32)).astype(BF16)
    group = place_of[0]
    col = place_of[1]
    panel_row = jnp.logical_and(t == 0, group < WIDE // BE)
    width = out.shape[1]
    step = WIDE if width % WIDE == 0 else 2 * BE
    for at in range(0, width, step):
        cols = slice(at, at + step)
        ch = col_high[cols, :]
        cl = col_low[cols, :]
        total = lax.dot_general(high, ch, dims, preferred_element_type=F32)
        total += lax.dot_general(high, cl, dims, preferred_element_type=F32)
        total += lax.dot_general(low, ch, dims, preferred_element_type=F32)
        value = front[:, cols] - total
        out[:, cols] = jnp.where(panel_row, 0.0, value)

    @pl.when(col < WIDE // BE)
    def _():
        at = pl.multiple_of(jnp.minimum(col, WIDE // BE - 1) * BE, BE)
        out[:, :BE] = lrow[:, pl.ds(at, BE)]


def update(front, lrow, lcol, place_of):
    rows, cols = front.shape
    return pl.pallas_call(
        update_kernel,
        grid_spec=pltpu.PrefetchScalarGridSpec(
            num_scalar_prefetch=1,
            grid=(rows // BE,),
            in_specs=[
                pl.BlockSpec((BE, cols), lambda t, *_: (t, 0)),
                pl.BlockSpec((BE, WIDE), lambda t, *_: (t, 0)),
                pl.BlockSpec((cols, WIDE), lambda t, *_: (0, 0)),
            ],
            out_specs=pl.BlockSpec((BE, cols), lambda t, *_: (t, 0)),
            scratch_shapes=[pltpu.VMEM((cols, WIDE), BF16), pltpu.VMEM((cols, WIDE), BF16)],
        ),
        out_shape=jax.ShapeDtypeStruct(front.shape, F32),
        compiler_params=pltpu.CompilerParams(vmem_limit_bytes=48 * 1024 * 1024),
        cost_estimate=pl.CostEstimate(
            flops=10_000_000_000, bytes_accessed=34_000_000, transcendentals=0
        ),
    )(place_of, front, lrow, lcol)


def child_tables(which_map, which_inner, grid_size, group_count, my_row, my_col, my_half, cap, slots):
    blocks_dev = slots * grid_size
    local_ids = jnp.arange(blocks_dev)
    residues = jnp.arange(grid_size)
    ids = local_ids[None, :] * grid_size + residues[:, None]
    targets = which_map[ids] % grid_size
    order = jnp.argsort(targets * blocks_dev + local_ids[None, :], axis=1)
    order = order.reshape(grid_size, grid_size, slots)
    row_ids = order[:, my_row, :] * grid_size + residues[:, None]
    col_ids = order[:, my_col, :] * grid_size + residues[:, None]
    row_blocks = which_map[row_ids]
    halves_of = row_blocks[:, 0] % group_count // grid_size

    def pick(target_half):
        hit = halves_of == target_half
        chosen = jnp.argsort(jnp.where(hit, 0, grid_size) + residues)[:cap]
        return chosen, hit[chosen]

    mine, valid = pick(my_half)
    other, _ = pick(1 - my_half)
    swapped = jnp.logical_not(
        use_direct(mine[:, None], residues[None, :], my_row, my_col)
    )
    lanes = jnp.arange(BE)
    row_perm = (which_inner[row_ids[mine]][:, :, None, :] == lanes[:, None]).astype(BF16)
    col_perm = (which_inner[col_ids][:, :, :, None] == lanes).astype(BF16)
    u_at = (which_map[col_ids] // grid_size).reshape(-1)
    return {
        "order": order,
        "mine": mine,
        "other": other,
        "valid": valid,
        "swapped": swapped.astype(jnp.int32).reshape(-1),
        "t_at": (row_blocks[mine] // group_count).reshape(-1),
        "u_at": u_at,
        "row_perm": row_perm,
        "col_perm": col_perm,
    }


def panel_column(received, rows, u_at, my_row, my_col, slots):
    side = slots * BE
    hit = u_at == 0
    found = jnp.any(hit)
    at = jnp.argmax(hit)
    s = at // slots
    k = at % slots
    pieces = []
    for a in range(rows.shape[0]):
        r = rows[a]
        straight = lax.dynamic_slice(received, (r, s, 0, k * BE), (1, 1, side, BE))[0, 0]
        across = lax.dynamic_slice(received, (r, s, k * BE, 0), (1, 1, BE, side))[0, 0]
        pieces.append(jnp.where(use_direct(r, s, my_row, my_col), straight, across.T))
    return jnp.where(found, jnp.stack(pieces), 0.0)


def panel_add(front_panel, columns, tables, slots):
    row_blocks = front_panel.shape[0]
    cap = columns.shape[0]
    at = jnp.argmax(tables["u_at"] == 0)
    col_perm = tables["col_perm"].reshape(-1, BE, BE)[at].astype(F32)
    blocks = columns.reshape(cap, slots, BE, BE)
    moved = jnp.einsum(
        "aixy,aiyz->aixz", tables["row_perm"].astype(F32), blocks, precision=HIGHEST
    )
    moved = jnp.dot(moved.reshape(-1, BE), col_perm, precision=HIGHEST).reshape(-1, BE, BE)
    t_of = jnp.where(jnp.repeat(tables["valid"], slots), tables["t_at"], -1)
    match = t_of[None, :] == jnp.arange(row_blocks)[:, None]
    picked = jnp.take(moved, jnp.argmax(match, axis=1), axis=0)
    return front_panel + jnp.where(jnp.any(match, axis=1)[:, None, None], picked, 0.0)


def on_device(front_init, child_update, child_map):
    grid_size = lax.axis_size("row")
    halves = lax.axis_size("half")
    group_count = halves * grid_size
    my_half = lax.axis_index("half")
    my_row = lax.axis_index("row")
    my_col = lax.axis_index("col")
    my_group = my_half * grid_size + my_row
    slots = child_update.shape[1] // BE // grid_size
    front_rows, front_cols = front_init.shape
    row_blocks = front_rows // BE
    cap = min(grid_size, row_blocks // slots)
    block_map = child_map.reshape(2, -1, BE)[:, :, 0] // BE
    inner_perm = child_map.reshape(2, -1, BE) % BE

    def tables(which):
        return child_tables(
            block_map[which], inner_perm[which], grid_size, group_count,
            my_row, my_col, my_half, cap, slots,
        )

    own = tables(my_half)
    far = tables(1 - my_half)

    packed = pack(
        child_update[0],
        own["order"][my_row].reshape(-1),
        own["order"][my_col].reshape(-1),
        grid_size,
        slots,
    )
    received = exchange(packed, grid_size)
    side = slots * BE

    swap_half = [(0, 1), (1, 0)]
    out_panel = panel_column(received, own["other"], own["u_at"], my_row, my_col, slots)
    far_panel = lax.ppermute(out_panel, "half", swap_half)
    outgoing = jnp.concatenate(
        [lax.dynamic_index_in_dim(received, own["other"][a], 0) for a in range(cap)], axis=0
    )
    outgoing, far_panel = lax.optimization_barrier((outgoing, far_panel))
    incoming = lax.ppermute(outgoing, "half", swap_half)

    own_panel = panel_column(received, own["mine"], own["u_at"], my_row, my_col, slots)
    panel = front_init[:, :BE].reshape(row_blocks, BE, BE)
    panel = panel_add(panel, own_panel, own, slots)
    panel = panel_add(panel, far_panel, far, slots)
    panel = panel.reshape(front_rows, BE)

    slab = lax.all_gather(panel, "col", axis=1, tiled=True)[:, :WIDE]
    diagonal = lax.all_gather(slab[:BE], ("half", "row"), axis=0, tiled=True)[:WIDE]
    pieces = []
    for k in range(grid_size):
        perm = [
            (a * grid_size + q, (q + k) % grid_size * grid_size + a)
            for a in range(grid_size)
            for q in range(grid_size)
        ]
        pieces.append(lax.ppermute(panel, ("row", "col"), perm))
    pieces = jnp.stack(pieces)
    pieces = jnp.take(pieces, (my_row - jnp.arange(WIDE // BE)) % grid_size, axis=0)
    near_rows = pieces.transpose(1, 0, 2).reshape(row_blocks, BE, WIDE)
    far_rows = lax.ppermute(near_rows, "half", swap_half)
    even = jnp.where(my_half == 0, near_rows, far_rows)
    odd = jnp.where(my_half == 0, far_rows, near_rows)
    column_side = jnp.stack([even, odd], axis=1).reshape(front_cols, WIDE)

    identity = jnp.eye(PANEL, dtype=F32)

    def inverse_of(block):
        factor = jnp.linalg.cholesky(block)
        return lax.linalg.triangular_solve(factor, identity, left_side=True, lower=True)

    inverse1 = inverse_of(diagonal[:PANEL, :PANEL])
    below = jnp.dot(diagonal[PANEL:, :PANEL], inverse1.T, precision=HIGHEST)
    inverse2 = inverse_of(
        diagonal[PANEL:, PANEL:] - jnp.dot(below, below.T, precision=HIGHEST)
    )

    def lower(rows, natural):
        first = jnp.dot(rows[:, :PANEL], inverse1.T, precision=HIGHEST)
        rest = rows[:, PANEL:] - jnp.dot(first, below.T, precision=HIGHEST)
        second = jnp.dot(rest, inverse2.T, precision=HIGHEST)
        second = jnp.where((natural >= PANEL)[:, None], second, 0.0)
        return jnp.concatenate([first, second], axis=1)

    row_ids = jnp.arange(front_rows)
    natural_rows = (row_ids // BE * group_count + my_group) * BE + row_ids % BE
    col_ids = jnp.arange(front_cols)
    natural_cols = (col_ids // BE * grid_size + my_col) * BE + col_ids % BE
    lrow = lower(slab, natural_rows)
    lcol = lower(column_side, natural_cols)

    residues = jnp.arange(grid_size)
    front = place(
        front_init,
        received.reshape(-1, side, side),
        (own["mine"][:, None] * grid_size + residues).reshape(-1),
        own["t_at"], own["u_at"], own["swapped"], own["valid"].astype(jnp.int32),
        own["row_perm"], own["col_perm"], grid_size,
    )
    front = place(
        front,
        incoming.reshape(-1, side, side),
        jnp.arange(cap * grid_size),
        far["t_at"], far["u_at"], far["swapped"], far["valid"].astype(jnp.int32),
        far["row_perm"], far["col_perm"], grid_size,
    )
    place_of = jnp.stack([my_group, my_col]).astype(jnp.int32)
    return update(front, lrow, lcol, place_of)


def solution(mesh):
    placed = (P(("half", "row"), "col"), P("half", "row", "col"), P())
    return jax.shard_map(
        on_device, mesh=mesh, in_specs=placed, out_specs=P(("half", "row"), "col"), check_vma=False
    )
```

```python
import functools

import jax
import jax.numpy as jnp
from jax import lax
from jax.experimental import pallas as pl
from jax.experimental.pallas import tpu as pltpu
from jax.sharding import PartitionSpec as P

BE = 128
PANEL = 256
WIDE = 512
HIGHEST = lax.Precision.HIGHEST
F32 = jnp.float32
BF16 = jnp.bfloat16


def absdiff(a, b):
    return jnp.maximum(a - b, b - a)


def use_direct(a, b, x, y):
    direct = 2 * absdiff(a, x) + absdiff(b // 2, y // 2)
    swapped = 2 * absdiff(b, x) + absdiff(a // 2, y // 2)
    return direct <= swapped


def pack_kernel(grid_size, slots, row_order, col_order, src, dst):
    for y in range(grid_size):
        for k in range(slots):
            at = pl.multiple_of(col_order[y * slots + k] * BE, BE)
            dst[0, y, :, k * BE : (k + 1) * BE] = src[:, pl.ds(at, BE)]


def pack(child, row_order, col_order, grid_size, slots):
    rows, cols = child.shape
    side = slots * BE
    return pl.pallas_call(
        functools.partial(pack_kernel, grid_size, slots),
        grid_spec=pltpu.PrefetchScalarGridSpec(
            num_scalar_prefetch=2,
            grid=(grid_size * slots,),
            in_specs=[pl.BlockSpec((BE, cols), lambda n, ro, co: (ro[n], 0))],
            out_specs=pl.BlockSpec(
                (1, grid_size, BE, side), lambda n, ro, co: (n // slots, 0, n % slots, 0)
            ),
        ),
        out_shape=jax.ShapeDtypeStruct((grid_size, grid_size, side, side), F32),
    )(row_order, col_order, child)


def exchange_kernel(
    grid_size, src, dst, relay, send_direct, send_swap, recv, local,
    relay_recv, relay_send,
):
    r = lax.axis_index("row")
    s = lax.axis_index("col")
    half = lax.axis_index("half")
    g = grid_size

    def peer(k):
        return (r + k // g) % g, (s + k % g) % g

    barrier = pltpu.get_barrier_semaphore()

    def greet(k, carry):
        x, y = peer(k)
        pl.semaphore_signal(
            barrier, inc=1, device_id=(half, x, y), device_id_type=pl.DeviceIdType.MESH
        )
        return carry

    lax.fori_loop(1, g * g, greet, 0)
    pl.semaphore_wait(barrier, g * g - 1)

    own = pltpu.make_async_copy(src.at[r, s], dst.at[r, s], local.at[0])
    own_swap = pltpu.make_async_copy(src.at[s, r], dst.at[s, r], local.at[1])
    own.start()

    @pl.when(r != s)
    def _():
        own_swap.start()

    def turns(x, y):
        return jnp.logical_and(x != r, y // 2 != s // 2)

    def first_hop(kind, k, x, y):
        source = src.at[y, x] if kind else src.at[x, y]
        return pltpu.make_async_remote_copy(
            src_ref=source,
            dst_ref=relay.at[s, x, kind],
            send_sem=(send_swap if kind else send_direct).at[k],
            recv_sem=relay_recv.at[(s * g + x) * 2 + kind],
            device_id=(half, r, y),
            device_id_type=pl.DeviceIdType.MESH,
        )

    def second_hop(kind, b, x):
        at = (b * g + x) * 2 + kind
        target, slot = (dst.at[b, r], b * g + r) if kind else (dst.at[r, b], r * g + b)
        return pltpu.make_async_remote_copy(
            src_ref=relay.at[b, x, kind],
            dst_ref=target,
            send_sem=relay_send.at[at],
            recv_sem=recv.at[slot],
            device_id=(half, x, s),
            device_id_type=pl.DeviceIdType.MESH,
        )

    def whole_way(kind, k, x, y):
        source, target, slot = (
            (src.at[y, x], dst.at[s, r], s * g + r)
            if kind
            else (src.at[x, y], dst.at[r, s], r * g + s)
        )
        return pltpu.make_async_remote_copy(
            src_ref=source,
            dst_ref=target,
            send_sem=(send_swap if kind else send_direct).at[k],
            recv_sem=recv.at[slot],
            device_id=(half, x, y),
            device_id_type=pl.DeviceIdType.MESH,
        )

    def wanted(kind, a, b, x, y):
        if kind:
            return jnp.logical_not(use_direct(b, a, x, y))
        return use_direct(a, b, x, y)

    def send_turning(k, carry):
        x, y = peer(k)
        for kind in range(2):

            @pl.when(jnp.logical_and(turns(x, y), wanted(kind, r, s, x, y)))
            def _():
                first_hop(kind, k, x, y).start()

        return carry

    lax.fori_loop(1, g * g, send_turning, 0)

    def send_straight(k, carry):
        x, y = peer(k)
        for kind in range(2):

            @pl.when(
                jnp.logical_and(
                    jnp.logical_not(turns(x, y)), wanted(kind, r, s, x, y)
                )
            )
            def _():
                whole_way(kind, k, x, y).start()

        return carry

    lax.fori_loop(1, g * g, send_straight, 0)

    def relayed(k):
        x = (r + k // g) % g
        b = (s + g - k % g) % g
        return b, x

    def pass_on(k, carry):
        b, x = relayed(k)
        for kind in range(2):

            @pl.when(
                jnp.logical_and(
                    jnp.logical_and(x != r, b // 2 != s // 2), wanted(kind, r, b, x, s)
                )
            )
            def _():
                pltpu.make_async_remote_copy(
                    src_ref=src.at[x, b],
                    dst_ref=relay.at[b, x, kind],
                    send_sem=send_direct.at[0],
                    recv_sem=relay_recv.at[(b * g + x) * 2 + kind],
                    device_id=(half, r, (s + 1) % g),
                    device_id_type=pl.DeviceIdType.MESH,
                ).wait_recv()
                second_hop(kind, b, x).start()

        return carry

    lax.fori_loop(1, g * g, pass_on, 0)

    def passed_on(k, carry):
        b, x = relayed(k)
        for kind in range(2):

            @pl.when(
                jnp.logical_and(
                    jnp.logical_and(x != r, b // 2 != s // 2), wanted(kind, r, b, x, s)
                )
            )
            def _():
                second_hop(kind, b, x).wait_send()

        return carry

    lax.fori_loop(1, g * g, passed_on, 0)

    def sent(k, carry):
        x, y = peer(k)
        for kind in range(2):

            @pl.when(wanted(kind, r, s, x, y))
            def _():
                whole_way(kind, k, x, y).wait_send()

        return carry

    lax.fori_loop(1, g * g, sent, 0)

    def arrived(k, carry):
        a = k // g
        b = k % g
        mine = jnp.logical_or(
            jnp.logical_and(a == r, b == s), jnp.logical_and(a == s, b == r)
        )

        @pl.when(jnp.logical_not(mine))
        def _():
            pltpu.make_async_remote_copy(
                src_ref=src.at[a, b],
                dst_ref=dst.at[a, b],
                send_sem=send_direct.at[0],
                recv_sem=recv.at[k],
                device_id=(half, (r + 1) % g, s),
                device_id_type=pl.DeviceIdType.MESH,
            ).wait_recv()

        return carry

    lax.fori_loop(0, g * g, arrived, 0)
    own.wait()

    @pl.when(r != s)
    def _():
        own_swap.wait()


def exchange(packed, grid_size):
    n = grid_size * grid_size
    return pl.pallas_call(
        functools.partial(exchange_kernel, grid_size),
        out_shape=[
            jax.ShapeDtypeStruct(packed.shape, F32),
            jax.ShapeDtypeStruct((grid_size, grid_size, 2) + packed.shape[2:], F32),
        ],
        in_specs=[pl.BlockSpec(memory_space=pl.ANY)],
        out_specs=[pl.BlockSpec(memory_space=pl.ANY)] * 2,
        scratch_shapes=[
            pltpu.SemaphoreType.DMA((n,)),
            pltpu.SemaphoreType.DMA((n,)),
            pltpu.SemaphoreType.DMA((n,)),
            pltpu.SemaphoreType.DMA((2,)),
            pltpu.SemaphoreType.DMA((2 * n,)),
            pltpu.SemaphoreType.DMA((2 * n,)),
        ],
        compiler_params=pltpu.CompilerParams(collective_id=0, has_side_effects=True),
    )(packed)[0]


def place_kernel(
    grid_size, slots, steps, chunk_at, t_at, u_at, swapped, valid,
    front, chunk, row_perm, col_perm, out, acc, work, mid, sem,
):
    n = pl.program_id(0)
    a = n // grid_size
    s = n % grid_size

    @pl.when(n == 0)
    def _():
        load = pltpu.make_async_copy(front, acc, sem)
        load.start()
        load.wait()

    @pl.when(valid[a] == 1)
    def _():
        @pl.when(swapped[n] == 1)
        def _():
            work[...] = chunk[0].T

        @pl.when(swapped[n] == 0)
        def _():
            work[...] = chunk[0]

        for i in range(slots):
            t = pl.multiple_of(t_at[a * slots + i] * BE, BE)
            part = work[i * BE : (i + 1) * BE, :]
            high = part.astype(BF16)
            low = (part - high.astype(F32)).astype(BF16)
            perm = row_perm[0, i]
            mid[0] = jnp.dot(perm, high, preferred_element_type=F32).astype(BF16)
            mid[1] = jnp.dot(perm, low, preferred_element_type=F32).astype(BF16)
            for k in range(slots):
                u = pl.multiple_of(u_at[s * slots + k] * BE, BE)
                lanes = slice(k * BE, (k + 1) * BE)
                both = jnp.concatenate([mid[0, :, lanes], mid[1, :, lanes]], axis=1)
                perm2 = jnp.concatenate([col_perm[0, k], col_perm[0, k]], axis=0)
                acc[pl.ds(t, BE), pl.ds(u, BE)] += jnp.dot(
                    both, perm2, preferred_element_type=F32
                )

    @pl.when(n == steps - 1)
    def _():
        store = pltpu.make_async_copy(acc, out, sem)
        store.start()
        store.wait()


def place(front, chunks, chunk_at, t_at, u_at, swapped, valid, row_perm, col_perm, grid_size):
    slots = row_perm.shape[1]
    steps = row_perm.shape[0] * grid_size
    side = slots * BE
    return pl.pallas_call(
        functools.partial(place_kernel, grid_size, slots, steps),
        grid_spec=pltpu.PrefetchScalarGridSpec(
            num_scalar_prefetch=5,
            grid=(steps,),
            in_specs=[
                pl.BlockSpec(memory_space=pl.ANY),
                pl.BlockSpec((1, side, side), lambda n, ca, *_: (ca[n], 0, 0)),
                pl.BlockSpec((1, slots, BE, BE), lambda n, *_: (n // grid_size, 0, 0, 0)),
                pl.BlockSpec((1, slots, BE, BE), lambda n, *_: (n % grid_size, 0, 0, 0)),
            ],
            out_specs=pl.BlockSpec(memory_space=pl.ANY),
            scratch_shapes=[
                pltpu.VMEM(front.shape, F32),
                pltpu.VMEM((side, side), F32),
                pltpu.VMEM((2, BE, side), BF16),
                pltpu.SemaphoreType.DMA,
            ],
        ),
        out_shape=jax.ShapeDtypeStruct(front.shape, F32),
        compiler_params=pltpu.CompilerParams(vmem_limit_bytes=40 * 1024 * 1024),
        cost_estimate=pl.CostEstimate(
            flops=4_000_000_000, bytes_accessed=36_000_000, transcendentals=0
        ),
    )(chunk_at, t_at, u_at, swapped, valid, front, chunks, row_perm, col_perm)


def update_kernel(place_of, front, lrow, lcol, out, col_high, col_low):
    t = pl.program_id(0)
    dims = (((1,), (1,)), ((), ()))

    @pl.when(t == 0)
    def _():
        whole = lcol[...]
        high = whole.astype(BF16)
        col_high[...] = high
        col_low[...] = (whole - high.astype(F32)).astype(BF16)

    rows = lrow[...]
    high = rows.astype(BF16)
    low = (rows - high.astype(F32)).astype(BF16)
    group = place_of[0]
    col = place_of[1]
    panel_row = jnp.logical_and(t == 0, group < WIDE // BE)
    width = out.shape[1]
    step = WIDE if width % WIDE == 0 else 2 * BE
    for at in range(0, width, step):
        cols = slice(at, at + step)
        ch = col_high[cols, :]
        cl = col_low[cols, :]
        total = lax.dot_general(high, ch, dims, preferred_element_type=F32)
        total += lax.dot_general(high, cl, dims, preferred_element_type=F32)
        total += lax.dot_general(low, ch, dims, preferred_element_type=F32)
        value = front[:, cols] - total
        out[:, cols] = jnp.where(panel_row, 0.0, value)

    @pl.when(col < WIDE // BE)
    def _():
        at = pl.multiple_of(jnp.minimum(col, WIDE // BE - 1) * BE, BE)
        out[:, :BE] = lrow[:, pl.ds(at, BE)]


def update(front, lrow, lcol, place_of):
    rows, cols = front.shape
    return pl.pallas_call(
        update_kernel,
        grid_spec=pltpu.PrefetchScalarGridSpec(
            num_scalar_prefetch=1,
            grid=(rows // BE,),
            in_specs=[
                pl.BlockSpec((BE, cols), lambda t, *_: (t, 0)),
                pl.BlockSpec((BE, WIDE), lambda t, *_: (t, 0)),
                pl.BlockSpec((cols, WIDE), lambda t, *_: (0, 0)),
            ],
            out_specs=pl.BlockSpec((BE, cols), lambda t, *_: (t, 0)),
            scratch_shapes=[pltpu.VMEM((cols, WIDE), BF16), pltpu.VMEM((cols, WIDE), BF16)],
        ),
        out_shape=jax.ShapeDtypeStruct(front.shape, F32),
        compiler_params=pltpu.CompilerParams(vmem_limit_bytes=48 * 1024 * 1024),
        cost_estimate=pl.CostEstimate(
            flops=10_000_000_000, bytes_accessed=34_000_000, transcendentals=0
        ),
    )(place_of, front, lrow, lcol)


def child_tables(which_map, which_inner, grid_size, group_count, my_row, my_col, my_half, cap, slots):
    blocks_dev = slots * grid_size
    local_ids = jnp.arange(blocks_dev)
    residues = jnp.arange(grid_size)
    ids = local_ids[None, :] * grid_size + residues[:, None]
    targets = which_map[ids] % grid_size
    order = jnp.argsort(targets * blocks_dev + local_ids[None, :], axis=1)
    order = order.reshape(grid_size, grid_size, slots)
    row_ids = order[:, my_row, :] * grid_size + residues[:, None]
    col_ids = order[:, my_col, :] * grid_size + residues[:, None]
    row_blocks = which_map[row_ids]
    halves_of = row_blocks[:, 0] % group_count // grid_size

    def pick(target_half):
        hit = halves_of == target_half
        chosen = jnp.argsort(jnp.where(hit, 0, grid_size) + residues)[:cap]
        return chosen, hit[chosen]

    mine, valid = pick(my_half)
    other, _ = pick(1 - my_half)
    swapped = jnp.logical_not(
        use_direct(mine[:, None], residues[None, :], my_row, my_col)
    )
    lanes = jnp.arange(BE)
    row_perm = (which_inner[row_ids[mine]][:, :, None, :] == lanes[:, None]).astype(BF16)
    col_perm = (which_inner[col_ids][:, :, :, None] == lanes).astype(BF16)
    u_at = (which_map[col_ids] // grid_size).reshape(-1)
    return {
        "order": order,
        "mine": mine,
        "other": other,
        "valid": valid,
        "swapped": swapped.astype(jnp.int32).reshape(-1),
        "t_at": (row_blocks[mine] // group_count).reshape(-1),
        "u_at": u_at,
        "row_perm": row_perm,
        "col_perm": col_perm,
    }


def panel_column(received, rows, u_at, my_row, my_col, slots):
    side = slots * BE
    hit = u_at == 0
    found = jnp.any(hit)
    at = jnp.argmax(hit)
    s = at // slots
    k = at % slots
    pieces = []
    for a in range(rows.shape[0]):
        r = rows[a]
        straight = lax.dynamic_slice(received, (r, s, 0, k * BE), (1, 1, side, BE))[0, 0]
        across = lax.dynamic_slice(received, (r, s, k * BE, 0), (1, 1, BE, side))[0, 0]
        pieces.append(jnp.where(use_direct(r, s, my_row, my_col), straight, across.T))
    return jnp.where(found, jnp.stack(pieces), 0.0)


def panel_add(front_panel, columns, tables, slots):
    row_blocks = front_panel.shape[0]
    cap = columns.shape[0]
    at = jnp.argmax(tables["u_at"] == 0)
    col_perm = tables["col_perm"].reshape(-1, BE, BE)[at].astype(F32)
    blocks = columns.reshape(cap, slots, BE, BE)
    moved = jnp.einsum(
        "aixy,aiyz->aixz", tables["row_perm"].astype(F32), blocks, precision=HIGHEST
    )
    moved = jnp.dot(moved.reshape(-1, BE), col_perm, precision=HIGHEST).reshape(-1, BE, BE)
    t_of = jnp.where(jnp.repeat(tables["valid"], slots), tables["t_at"], -1)
    match = t_of[None, :] == jnp.arange(row_blocks)[:, None]
    picked = jnp.take(moved, jnp.argmax(match, axis=1), axis=0)
    return front_panel + jnp.where(jnp.any(match, axis=1)[:, None, None], picked, 0.0)


def on_device(front_init, child_update, child_map):
    grid_size = lax.axis_size("row")
    halves = lax.axis_size("half")
    group_count = halves * grid_size
    my_half = lax.axis_index("half")
    my_row = lax.axis_index("row")
    my_col = lax.axis_index("col")
    my_group = my_half * grid_size + my_row
    slots = child_update.shape[1] // BE // grid_size
    front_rows, front_cols = front_init.shape
    row_blocks = front_rows // BE
    cap = min(grid_size, row_blocks // slots)
    block_map = child_map.reshape(2, -1, BE)[:, :, 0] // BE
    inner_perm = child_map.reshape(2, -1, BE) % BE

    def tables(which):
        return child_tables(
            block_map[which], inner_perm[which], grid_size, group_count,
            my_row, my_col, my_half, cap, slots,
        )

    own = tables(my_half)
    far = tables(1 - my_half)

    packed = pack(
        child_update[0],
        own["order"][my_row].reshape(-1),
        own["order"][my_col].reshape(-1),
        grid_size,
        slots,
    )
    received = exchange(packed, grid_size)
    side = slots * BE

    swap_half = [(0, 1), (1, 0)]
    out_panel = panel_column(received, own["other"], own["u_at"], my_row, my_col, slots)
    far_panel = lax.ppermute(out_panel, "half", swap_half)
    outgoing = jnp.concatenate(
        [lax.dynamic_index_in_dim(received, own["other"][a], 0) for a in range(cap)], axis=0
    )
    outgoing, far_panel = lax.optimization_barrier((outgoing, far_panel))
    incoming = lax.ppermute(outgoing, "half", swap_half)

    own_panel = panel_column(received, own["mine"], own["u_at"], my_row, my_col, slots)
    panel = front_init[:, :BE].reshape(row_blocks, BE, BE)
    panel = panel_add(panel, own_panel, own, slots)
    panel = panel_add(panel, far_panel, far, slots)
    panel = panel.reshape(front_rows, BE)

    slab = lax.all_gather(panel, "col", axis=1, tiled=True)[:, :WIDE]
    diagonal = lax.all_gather(slab[:BE], ("half", "row"), axis=0, tiled=True)[:WIDE]
    pieces = []
    for k in range(grid_size):
        perm = [
            (a * grid_size + q, (q + k) % grid_size * grid_size + a)
            for a in range(grid_size)
            for q in range(grid_size)
        ]
        pieces.append(lax.ppermute(panel, ("row", "col"), perm))
    pieces = jnp.stack(pieces)
    pieces = jnp.take(pieces, (my_row - jnp.arange(WIDE // BE)) % grid_size, axis=0)
    near_rows = pieces.transpose(1, 0, 2).reshape(row_blocks, BE, WIDE)
    far_rows = lax.ppermute(near_rows, "half", swap_half)
    even = jnp.where(my_half == 0, near_rows, far_rows)
    odd = jnp.where(my_half == 0, far_rows, near_rows)
    column_side = jnp.stack([even, odd], axis=1).reshape(front_cols, WIDE)

    identity = jnp.eye(BE, dtype=F32)
    block_of = jnp.arange(WIDE) // BE

    def eliminate(k, carry):
        schur, inverse = carry
        at = k * BE
        block = lax.dynamic_slice(schur, (at, at), (BE, BE))
        factor = lax.linalg.cholesky(block, symmetrize_input=False)
        small = lax.linalg.triangular_solve(factor, identity, left_side=True, lower=True)
        below = jnp.dot(
            lax.dynamic_slice(schur, (0, at), (WIDE, BE)), small.T, precision=HIGHEST
        )
        below = jnp.where((block_of > k)[:, None], below, 0.0)
        schur = schur - jnp.dot(below, below.T, precision=HIGHEST)
        mine = jnp.dot(
            small, lax.dynamic_slice(inverse, (at, 0), (BE, WIDE)), precision=HIGHEST
        )
        inverse = inverse - jnp.dot(below, mine, precision=HIGHEST)
        return schur, lax.dynamic_update_slice(inverse, mine, (at, 0))

    _, inverse = lax.fori_loop(0, WIDE // BE, eliminate, (diagonal, jnp.eye(WIDE, dtype=F32)))

    def lower(rows, natural):
        full = jnp.dot(rows, inverse.T, precision=HIGHEST)
        second = (jnp.arange(WIDE) >= PANEL)[None, :] & (natural < PANEL)[:, None]
        return jnp.where(second, 0.0, full)

    row_ids = jnp.arange(front_rows)
    natural_rows = (row_ids // BE * group_count + my_group) * BE + row_ids % BE
    col_ids = jnp.arange(front_cols)
    natural_cols = (col_ids // BE * grid_size + my_col) * BE + col_ids % BE
    lrow = lower(slab, natural_rows)
    lcol = lower(column_side, natural_cols)

    residues = jnp.arange(grid_size)
    front = place(
        front_init,
        received.reshape(-1, side, side),
        (own["mine"][:, None] * grid_size + residues).reshape(-1),
        own["t_at"], own["u_at"], own["swapped"], own["valid"].astype(jnp.int32),
        own["row_perm"], own["col_perm"], grid_size,
    )
    front = place(
        front,
        incoming.reshape(-1, side, side),
        jnp.arange(cap * grid_size),
        far["t_at"], far["u_at"], far["swapped"], far["valid"].astype(jnp.int32),
        far["row_perm"], far["col_perm"], grid_size,
    )
    place_of = jnp.stack([my_group, my_col]).astype(jnp.int32)
    return update(front, lrow, lcol, place_of)


def solution(mesh):
    placed = (P(("half", "row"), "col"), P("half", "row", "col"), P())
    return jax.shard_map(
        on_device, mesh=mesh, in_specs=placed, out_specs=P(("half", "row"), "col"), check_vma=False
    )
```

```python
import functools

import jax
import jax.numpy as jnp
from jax import lax
from jax.experimental import pallas as pl
from jax.experimental.pallas import tpu as pltpu
from jax.sharding import PartitionSpec as P

BE = 128
PANEL = 256
WIDE = 512
HIGHEST = lax.Precision.HIGHEST
F32 = jnp.float32
BF16 = jnp.bfloat16


def absdiff(a, b):
    return jnp.maximum(a - b, b - a)


def use_direct(a, b, x, y):
    direct = 2 * absdiff(a, x) + absdiff(b // 2, y // 2)
    swapped = 2 * absdiff(b, x) + absdiff(a // 2, y // 2)
    return direct <= swapped


def pack_kernel(grid_size, slots, row_order, col_order, src, dst):
    for y in range(grid_size):
        for k in range(slots):
            at = pl.multiple_of(col_order[y * slots + k] * BE, BE)
            dst[0, y, :, k * BE : (k + 1) * BE] = src[:, pl.ds(at, BE)]


def pack(child, row_order, col_order, grid_size, slots):
    rows, cols = child.shape
    side = slots * BE
    return pl.pallas_call(
        functools.partial(pack_kernel, grid_size, slots),
        grid_spec=pltpu.PrefetchScalarGridSpec(
            num_scalar_prefetch=2,
            grid=(grid_size * slots,),
            in_specs=[pl.BlockSpec((BE, cols), lambda n, ro, co: (ro[n], 0))],
            out_specs=pl.BlockSpec(
                (1, grid_size, BE, side), lambda n, ro, co: (n // slots, 0, n % slots, 0)
            ),
        ),
        out_shape=jax.ShapeDtypeStruct((grid_size, grid_size, side, side), F32),
    )(row_order, col_order, child)


def exchange_kernel(
    grid_size, src, dst, relay, send_direct, send_swap, recv, local,
    relay_recv, relay_send,
):
    r = lax.axis_index("row")
    s = lax.axis_index("col")
    half = lax.axis_index("half")
    g = grid_size

    def peer(k):
        return (r + k // g) % g, (s + k % g) % g

    barrier = pltpu.get_barrier_semaphore()

    def greet(k, carry):
        x, y = peer(k)
        pl.semaphore_signal(
            barrier, inc=1, device_id=(half, x, y), device_id_type=pl.DeviceIdType.MESH
        )
        return carry

    lax.fori_loop(1, g * g, greet, 0)
    pl.semaphore_wait(barrier, g * g - 1)

    own = pltpu.make_async_copy(src.at[r, s], dst.at[r, s], local.at[0])
    own_swap = pltpu.make_async_copy(src.at[s, r], dst.at[s, r], local.at[1])
    own.start()

    @pl.when(r != s)
    def _():
        own_swap.start()

    def turns(x, y):
        return jnp.logical_and(x != r, y // 2 != s // 2)

    def first_hop(kind, k, x, y):
        source = src.at[y, x] if kind else src.at[x, y]
        return pltpu.make_async_remote_copy(
            src_ref=source,
            dst_ref=relay.at[s, x, kind],
            send_sem=(send_swap if kind else send_direct).at[k],
            recv_sem=relay_recv.at[(s * g + x) * 2 + kind],
            device_id=(half, r, y),
            device_id_type=pl.DeviceIdType.MESH,
        )

    def second_hop(kind, b, x):
        at = (b * g + x) * 2 + kind
        target, slot = (dst.at[b, r], b * g + r) if kind else (dst.at[r, b], r * g + b)
        return pltpu.make_async_remote_copy(
            src_ref=relay.at[b, x, kind],
            dst_ref=target,
            send_sem=relay_send.at[at],
            recv_sem=recv.at[slot],
            device_id=(half, x, s),
            device_id_type=pl.DeviceIdType.MESH,
        )

    def whole_way(kind, k, x, y):
        source, target, slot = (
            (src.at[y, x], dst.at[s, r], s * g + r)
            if kind
            else (src.at[x, y], dst.at[r, s], r * g + s)
        )
        return pltpu.make_async_remote_copy(
            src_ref=source,
            dst_ref=target,
            send_sem=(send_swap if kind else send_direct).at[k],
            recv_sem=recv.at[slot],
            device_id=(half, x, y),
            device_id_type=pl.DeviceIdType.MESH,
        )

    def wanted(kind, a, b, x, y):
        if kind:
            return jnp.logical_not(use_direct(b, a, x, y))
        return use_direct(a, b, x, y)

    def send_turning(k, carry):
        x, y = peer(k)
        for kind in range(2):

            @pl.when(jnp.logical_and(turns(x, y), wanted(kind, r, s, x, y)))
            def _():
                first_hop(kind, k, x, y).start()

        return carry

    lax.fori_loop(1, g * g, send_turning, 0)

    def send_straight(k, carry):
        x, y = peer(k)
        for kind in range(2):

            @pl.when(
                jnp.logical_and(
                    jnp.logical_not(turns(x, y)), wanted(kind, r, s, x, y)
                )
            )
            def _():
                whole_way(kind, k, x, y).start()

        return carry

    lax.fori_loop(1, g * g, send_straight, 0)

    def relayed(k):
        x = (r + k // g) % g
        b = (s + g - k % g) % g
        return b, x

    def pass_on(k, carry):
        b, x = relayed(k)
        for kind in range(2):

            @pl.when(
                jnp.logical_and(
                    jnp.logical_and(x != r, b // 2 != s // 2), wanted(kind, r, b, x, s)
                )
            )
            def _():
                pltpu.make_async_remote_copy(
                    src_ref=src.at[x, b],
                    dst_ref=relay.at[b, x, kind],
                    send_sem=send_direct.at[0],
                    recv_sem=relay_recv.at[(b * g + x) * 2 + kind],
                    device_id=(half, r, (s + 1) % g),
                    device_id_type=pl.DeviceIdType.MESH,
                ).wait_recv()
                second_hop(kind, b, x).start()

        return carry

    lax.fori_loop(1, g * g, pass_on, 0)

    def passed_on(k, carry):
        b, x = relayed(k)
        for kind in range(2):

            @pl.when(
                jnp.logical_and(
                    jnp.logical_and(x != r, b // 2 != s // 2), wanted(kind, r, b, x, s)
                )
            )
            def _():
                second_hop(kind, b, x).wait_send()

        return carry

    lax.fori_loop(1, g * g, passed_on, 0)

    def sent(k, carry):
        x, y = peer(k)
        for kind in range(2):

            @pl.when(wanted(kind, r, s, x, y))
            def _():
                whole_way(kind, k, x, y).wait_send()

        return carry

    lax.fori_loop(1, g * g, sent, 0)

    def arrived(k, carry):
        a = k // g
        b = k % g
        mine = jnp.logical_or(
            jnp.logical_and(a == r, b == s), jnp.logical_and(a == s, b == r)
        )

        @pl.when(jnp.logical_not(mine))
        def _():
            pltpu.make_async_remote_copy(
                src_ref=src.at[a, b],
                dst_ref=dst.at[a, b],
                send_sem=send_direct.at[0],
                recv_sem=recv.at[k],
                device_id=(half, (r + 1) % g, s),
                device_id_type=pl.DeviceIdType.MESH,
            ).wait_recv()

        return carry

    lax.fori_loop(0, g * g, arrived, 0)
    own.wait()

    @pl.when(r != s)
    def _():
        own_swap.wait()


def exchange(packed, grid_size):
    n = grid_size * grid_size
    return pl.pallas_call(
        functools.partial(exchange_kernel, grid_size),
        out_shape=[
            jax.ShapeDtypeStruct(packed.shape, F32),
            jax.ShapeDtypeStruct((grid_size, grid_size, 2) + packed.shape[2:], F32),
        ],
        in_specs=[pl.BlockSpec(memory_space=pl.ANY)],
        out_specs=[pl.BlockSpec(memory_space=pl.ANY)] * 2,
        scratch_shapes=[
            pltpu.SemaphoreType.DMA((n,)),
            pltpu.SemaphoreType.DMA((n,)),
            pltpu.SemaphoreType.DMA((n,)),
            pltpu.SemaphoreType.DMA((2,)),
            pltpu.SemaphoreType.DMA((2 * n,)),
            pltpu.SemaphoreType.DMA((2 * n,)),
        ],
        compiler_params=pltpu.CompilerParams(collective_id=0, has_side_effects=True),
    )(packed)[0]


def place_kernel(
    grid_size, slots, steps, chunk_at, t_at, u_at, swapped, valid,
    front, row_perm, col_perm, *rest,
):
    *chunks, out, acc, work, mid, sem = rest
    n = pl.program_id(0)
    a = n // grid_size
    s = n % grid_size

    @pl.when(n == 0)
    def _():
        load = pltpu.make_async_copy(front, acc, sem)
        load.start()
        load.wait()

    @pl.when(valid[a] == 1)
    def _():
        for q, chunk in enumerate(chunks):
            here = a == q if len(chunks) > 1 else a >= 0

            @pl.when(jnp.logical_and(here, swapped[n] == 1))
            def _():
                work[...] = chunk[0].T

            @pl.when(jnp.logical_and(here, swapped[n] == 0))
            def _():
                work[...] = chunk[0]

        for i in range(slots):
            t = pl.multiple_of(t_at[a * slots + i] * BE, BE)
            part = work[i * BE : (i + 1) * BE, :]
            high = part.astype(BF16)
            low = (part - high.astype(F32)).astype(BF16)
            perm = row_perm[0, i]
            mid[0] = jnp.dot(perm, high, preferred_element_type=F32).astype(BF16)
            mid[1] = jnp.dot(perm, low, preferred_element_type=F32).astype(BF16)
            for k in range(slots):
                u = pl.multiple_of(u_at[s * slots + k] * BE, BE)
                lanes = slice(k * BE, (k + 1) * BE)
                both = jnp.concatenate([mid[0, :, lanes], mid[1, :, lanes]], axis=1)
                perm2 = jnp.concatenate([col_perm[0, k], col_perm[0, k]], axis=0)
                acc[pl.ds(t, BE), pl.ds(u, BE)] += jnp.dot(
                    both, perm2, preferred_element_type=F32
                )

    @pl.when(n == steps - 1)
    def _():
        store = pltpu.make_async_copy(acc, out, sem)
        store.start()
        store.wait()


def place(front, chunks, chunk_at, t_at, u_at, swapped, valid, row_perm, col_perm, grid_size):
    slots = row_perm.shape[1]
    steps = row_perm.shape[0] * grid_size
    side = slots * BE

    def chunk_spec(q):
        if len(chunks) == 1:
            return pl.BlockSpec((1, side, side), lambda n, ca, *_: (ca[n], 0, 0))
        return pl.BlockSpec(
            (1, side, side),
            lambda n, *_: (jnp.clip(n - q * grid_size, 0, grid_size - 1), 0, 0),
        )

    return pl.pallas_call(
        functools.partial(place_kernel, grid_size, slots, steps),
        grid_spec=pltpu.PrefetchScalarGridSpec(
            num_scalar_prefetch=5,
            grid=(steps,),
            in_specs=[
                pl.BlockSpec(memory_space=pl.ANY),
                pl.BlockSpec((1, slots, BE, BE), lambda n, *_: (n // grid_size, 0, 0, 0)),
                pl.BlockSpec((1, slots, BE, BE), lambda n, *_: (n % grid_size, 0, 0, 0)),
            ]
            + [chunk_spec(q) for q in range(len(chunks))],
            out_specs=pl.BlockSpec(memory_space=pl.ANY),
            scratch_shapes=[
                pltpu.VMEM(front.shape, F32),
                pltpu.VMEM((side, side), F32),
                pltpu.VMEM((2, BE, side), BF16),
                pltpu.SemaphoreType.DMA,
            ],
        ),
        out_shape=jax.ShapeDtypeStruct(front.shape, F32),
        compiler_params=pltpu.CompilerParams(vmem_limit_bytes=40 * 1024 * 1024),
        cost_estimate=pl.CostEstimate(
            flops=4_000_000_000, bytes_accessed=36_000_000, transcendentals=0
        ),
    )(chunk_at, t_at, u_at, swapped, valid, front, row_perm, col_perm, *chunks)


def update_kernel(place_of, front, lrow, lcol, out, col_high, col_low):
    t = pl.program_id(0)
    dims = (((1,), (1,)), ((), ()))

    @pl.when(t == 0)
    def _():
        whole = lcol[...]
        high = whole.astype(BF16)
        col_high[...] = high
        col_low[...] = (whole - high.astype(F32)).astype(BF16)

    rows = lrow[...]
    high = rows.astype(BF16)
    low = (rows - high.astype(F32)).astype(BF16)
    group = place_of[0]
    col = place_of[1]
    panel_row = jnp.logical_and(t == 0, group < WIDE // BE)
    width = out.shape[1]
    step = WIDE if width % WIDE == 0 else 2 * BE
    for at in range(0, width, step):
        cols = slice(at, at + step)
        ch = col_high[cols, :]
        cl = col_low[cols, :]
        total = lax.dot_general(high, ch, dims, preferred_element_type=F32)
        total += lax.dot_general(high, cl, dims, preferred_element_type=F32)
        total += lax.dot_general(low, ch, dims, preferred_element_type=F32)
        value = front[:, cols] - total
        out[:, cols] = jnp.where(panel_row, 0.0, value)

    @pl.when(col < WIDE // BE)
    def _():
        at = pl.multiple_of(jnp.minimum(col, WIDE // BE - 1) * BE, BE)
        out[:, :BE] = lrow[:, pl.ds(at, BE)]


def update(front, lrow, lcol, place_of):
    rows, cols = front.shape
    return pl.pallas_call(
        update_kernel,
        grid_spec=pltpu.PrefetchScalarGridSpec(
            num_scalar_prefetch=1,
            grid=(rows // BE,),
            in_specs=[
                pl.BlockSpec((BE, cols), lambda t, *_: (t, 0)),
                pl.BlockSpec((BE, WIDE), lambda t, *_: (t, 0)),
                pl.BlockSpec((cols, WIDE), lambda t, *_: (0, 0)),
            ],
            out_specs=pl.BlockSpec((BE, cols), lambda t, *_: (t, 0)),
            scratch_shapes=[pltpu.VMEM((cols, WIDE), BF16), pltpu.VMEM((cols, WIDE), BF16)],
        ),
        out_shape=jax.ShapeDtypeStruct(front.shape, F32),
        compiler_params=pltpu.CompilerParams(vmem_limit_bytes=48 * 1024 * 1024),
        cost_estimate=pl.CostEstimate(
            flops=10_000_000_000, bytes_accessed=34_000_000, transcendentals=0
        ),
    )(place_of, front, lrow, lcol)


def child_tables(which_map, which_inner, grid_size, group_count, my_row, my_col, my_half, cap, slots):
    blocks_dev = slots * grid_size
    local_ids = jnp.arange(blocks_dev)
    residues = jnp.arange(grid_size)
    ids = local_ids[None, :] * grid_size + residues[:, None]
    targets = which_map[ids] % grid_size
    order = jnp.argsort(targets * blocks_dev + local_ids[None, :], axis=1)
    order = order.reshape(grid_size, grid_size, slots)
    row_ids = order[:, my_row, :] * grid_size + residues[:, None]
    col_ids = order[:, my_col, :] * grid_size + residues[:, None]
    row_blocks = which_map[row_ids]
    halves_of = row_blocks[:, 0] % group_count // grid_size

    def pick(target_half):
        hit = halves_of == target_half
        chosen = jnp.argsort(jnp.where(hit, 0, grid_size) + residues)[:cap]
        return chosen, hit[chosen]

    mine, valid = pick(my_half)
    other, _ = pick(1 - my_half)
    swapped = jnp.logical_not(
        use_direct(mine[:, None], residues[None, :], my_row, my_col)
    )
    lanes = jnp.arange(BE)
    row_perm = (which_inner[row_ids[mine]][:, :, None, :] == lanes[:, None]).astype(BF16)
    col_perm = (which_inner[col_ids][:, :, :, None] == lanes).astype(BF16)
    u_at = (which_map[col_ids] // grid_size).reshape(-1)
    return {
        "order": order,
        "mine": mine,
        "other": other,
        "valid": valid,
        "swapped": swapped.astype(jnp.int32).reshape(-1),
        "t_at": (row_blocks[mine] // group_count).reshape(-1),
        "u_at": u_at,
        "row_perm": row_perm,
        "col_perm": col_perm,
    }


def panel_column(received, rows, u_at, my_row, my_col, slots):
    side = slots * BE
    hit = u_at == 0
    found = jnp.any(hit)
    at = jnp.argmax(hit)
    s = at // slots
    k = at % slots
    pieces = []
    for a in range(rows.shape[0]):
        r = rows[a]
        straight = lax.dynamic_slice(received, (r, s, 0, k * BE), (1, 1, side, BE))[0, 0]
        across = lax.dynamic_slice(received, (r, s, k * BE, 0), (1, 1, BE, side))[0, 0]
        pieces.append(jnp.where(use_direct(r, s, my_row, my_col), straight, across.T))
    return jnp.where(found, jnp.stack(pieces), 0.0)


def panel_add(front_panel, columns, tables, slots):
    row_blocks = front_panel.shape[0]
    cap = columns.shape[0]
    at = jnp.argmax(tables["u_at"] == 0)
    col_perm = tables["col_perm"].reshape(-1, BE, BE)[at].astype(F32)
    blocks = columns.reshape(cap, slots, BE, BE)
    moved = jnp.einsum(
        "aixy,aiyz->aixz", tables["row_perm"].astype(F32), blocks, precision=HIGHEST
    )
    moved = jnp.dot(moved.reshape(-1, BE), col_perm, precision=HIGHEST).reshape(-1, BE, BE)
    t_of = jnp.where(jnp.repeat(tables["valid"], slots), tables["t_at"], -1)
    match = t_of[None, :] == jnp.arange(row_blocks)[:, None]
    picked = jnp.take(moved, jnp.argmax(match, axis=1), axis=0)
    return front_panel + jnp.where(jnp.any(match, axis=1)[:, None, None], picked, 0.0)


def on_device(front_init, child_update, child_map):
    grid_size = lax.axis_size("row")
    halves = lax.axis_size("half")
    group_count = halves * grid_size
    my_half = lax.axis_index("half")
    my_row = lax.axis_index("row")
    my_col = lax.axis_index("col")
    my_group = my_half * grid_size + my_row
    slots = child_update.shape[1] // BE // grid_size
    front_rows, front_cols = front_init.shape
    row_blocks = front_rows // BE
    cap = min(grid_size, row_blocks // slots)
    block_map = child_map.reshape(2, -1, BE)[:, :, 0] // BE
    inner_perm = child_map.reshape(2, -1, BE) % BE

    def tables(which):
        return child_tables(
            block_map[which], inner_perm[which], grid_size, group_count,
            my_row, my_col, my_half, cap, slots,
        )

    own = tables(my_half)
    far = tables(1 - my_half)

    packed = pack(
        child_update[0],
        own["order"][my_row].reshape(-1),
        own["order"][my_col].reshape(-1),
        grid_size,
        slots,
    )
    received = exchange(packed, grid_size)
    side = slots * BE

    swap_half = [(0, 1), (1, 0)]
    out_panel = panel_column(received, own["other"], own["u_at"], my_row, my_col, slots)
    far_panel = lax.ppermute(out_panel, "half", swap_half)
    incoming = [
        lax.ppermute(
            lax.dynamic_index_in_dim(received, own["other"][a], 0, keepdims=False),
            "half",
            swap_half,
        )
        for a in range(cap)
    ]

    own_panel = panel_column(received, own["mine"], own["u_at"], my_row, my_col, slots)
    panel = front_init[:, :BE].reshape(row_blocks, BE, BE)
    panel = panel_add(panel, own_panel, own, slots)
    panel = panel_add(panel, far_panel, far, slots)
    panel = panel.reshape(front_rows, BE)

    slab = lax.all_gather(panel, "col", axis=1, tiled=True)[:, :WIDE]
    diagonal = lax.all_gather(slab[:BE], ("half", "row"), axis=0, tiled=True)[:WIDE]
    pieces = []
    for k in range(grid_size):
        perm = [
            (a * grid_size + q, (q + k) % grid_size * grid_size + a)
            for a in range(grid_size)
            for q in range(grid_size)
        ]
        pieces.append(lax.ppermute(panel, ("row", "col"), perm))
    pieces = jnp.stack(pieces)
    pieces = jnp.take(pieces, (my_row - jnp.arange(WIDE // BE)) % grid_size, axis=0)
    near_rows = pieces.transpose(1, 0, 2).reshape(row_blocks, BE, WIDE)
    far_rows = lax.ppermute(near_rows, "half", swap_half)
    even = jnp.where(my_half == 0, near_rows, far_rows)
    odd = jnp.where(my_half == 0, far_rows, near_rows)
    column_side = jnp.stack([even, odd], axis=1).reshape(front_cols, WIDE)

    identity = jnp.eye(BE, dtype=F32)
    block_of = jnp.arange(WIDE) // BE

    def eliminate(k, carry):
        schur, inverse = carry
        at = k * BE
        block = lax.dynamic_slice(schur, (at, at), (BE, BE))
        factor = lax.linalg.cholesky(block, symmetrize_input=False)
        small = lax.linalg.triangular_solve(factor, identity, left_side=True, lower=True)
        below = jnp.dot(
            lax.dynamic_slice(schur, (0, at), (WIDE, BE)), small.T, precision=HIGHEST
        )
        below = jnp.where((block_of > k)[:, None], below, 0.0)
        schur = schur - jnp.dot(below, below.T, precision=HIGHEST)
        mine = jnp.dot(
            small, lax.dynamic_slice(inverse, (at, 0), (BE, WIDE)), precision=HIGHEST
        )
        inverse = inverse - jnp.dot(below, mine, precision=HIGHEST)
        return schur, lax.dynamic_update_slice(inverse, mine, (at, 0))

    _, inverse = lax.fori_loop(0, WIDE // BE, eliminate, (diagonal, jnp.eye(WIDE, dtype=F32)))

    def lower(rows, natural):
        full = jnp.dot(rows, inverse.T, precision=HIGHEST)
        second = (jnp.arange(WIDE) >= PANEL)[None, :] & (natural < PANEL)[:, None]
        return jnp.where(second, 0.0, full)

    row_ids = jnp.arange(front_rows)
    natural_rows = (row_ids // BE * group_count + my_group) * BE + row_ids % BE
    col_ids = jnp.arange(front_cols)
    natural_cols = (col_ids // BE * grid_size + my_col) * BE + col_ids % BE
    lrow = lower(slab, natural_rows)
    lcol = lower(column_side, natural_cols)

    residues = jnp.arange(grid_size)
    front = place(
        front_init,
        [received.reshape(-1, side, side)],
        (own["mine"][:, None] * grid_size + residues).reshape(-1),
        own["t_at"], own["u_at"], own["swapped"], own["valid"].astype(jnp.int32),
        own["row_perm"], own["col_perm"], grid_size,
    )
    front = place(
        front,
        incoming,
        jnp.arange(cap * grid_size),
        far["t_at"], far["u_at"], far["swapped"], far["valid"].astype(jnp.int32),
        far["row_perm"], far["col_perm"], grid_size,
    )
    place_of = jnp.stack([my_group, my_col]).astype(jnp.int32)
    return update(front, lrow, lcol, place_of)


def solution(mesh):
    placed = (P(("half", "row"), "col"), P("half", "row", "col"), P())
    return jax.shard_map(
        on_device, mesh=mesh, in_specs=placed, out_specs=P(("half", "row"), "col"), check_vma=False
    )
```
